256 devices in a mesh: layer: 64 (over y, x_lo, z), feat: 4 (over x_hi, core).
Axes of the slice: x: 4 (x_hi: 2, x_lo: 2; x = x_hi * 2 + x_lo), y: 4, z: 8, core: 2. Of those that a mesh axis runs over, the one named last changes fastest.
Arguments:
- sources: bfloat16 [256, 8192], P(('layer', 'feat')), may hold values from -6 to 6
- targets: bfloat16 [256, 16384], P(('layer', 'feat')), may hold values from -16 to 16
- enc_weight: bfloat16 [8192, 32768], P(None, ('feat', 'layer')), may hold values from -0.0625 to 0.0625
- enc_bias: float32 [32768], P(('feat', 'layer')), may hold values from -3 to 3
- dec_weight: bfloat16 [32768, 16384], P('feat', 'layer'), may hold values from -0.03125 to 0.03125
- dec_bias: float32 [16384], P('layer'), may hold values from -3 to 3
Outputs:
- enc_grad: bfloat16 [8192, 32768], P(None, ('feat', 'layer'))
- dec_grad: bfloat16 [32768, 16384], P('feat', 'layer')
- mse: float32 [], replicated
The draws below stay inside these ranges and needn't reach their ends.
All inputs are finite; a program needn't handle non-finite values.
Results may differ from the reference program's by a relative error of at most 0.011.
Values may be sent and summed in bfloat16 or wider, within the bound.
No kernel may reach another device: no remote copies, remote signals or barrier semaphores. Data moves between devices by JAX's collectives and lax.ppermute only.
A program may use at most 128 MiB of HBM per device.

```python
import math
import jax
import jax.numpy as jnp
from jax import lax

D = 8192
F = 32768
TL = 2
TOKENS = 256


def draw_targets(key, part):
    columns = TL * D
    place = jnp.arange(columns, dtype=jnp.float32) / float(columns - 1)
    scale = jnp.exp(place * jnp.log(3.5))
    base = jnp.clip(jax.random.normal(key, (TOKENS, columns), jnp.float32), -4.0, 4.0)
    return (base * scale[None, :]).astype(jnp.bfloat16)


def level_of(rng, dims, shards, low, top_value):
    loudness, own = 1.0, jax.random.fold_in(rng, 6)
    for axis_at, shards_of in shards:
        heights = jnp.exp(jax.random.uniform(jax.random.fold_in(own, axis_at), (shards_of,), jnp.float32, low / len(shards), top_value / len(shards)))
        loudness = loudness * jnp.repeat(heights, dims[axis_at] // shards_of).reshape([-1 if axis == axis_at else 1 for axis in range(len(dims))])
    return loudness


def gaussian(key, dims, scale, limit, cuts=(), held_as=jnp.bfloat16):
    loudness = level_of(key, dims, cuts, -0.22, 0.18) if cuts else 1.0
    array = jax.random.normal(key, dims, jnp.float32) * scale * loudness
    return jnp.minimum(jnp.maximum(array, -limit), limit).astype(held_as)


def setup_inputs(seed: int = 0) -> dict:
    key_list = jax.random.split(jax.random.key(seed), 7)
    return {
        "sources": gaussian(key_list[0], (TOKENS, D), 1.0, 6.0, ((0, 256),)),
        "targets": draw_targets(jax.random.fold_in(key_list[6], 71), 0),
        "enc_weight": gaussian(key_list[2], (D, F), D ** -0.5, 0.0625, ((1, 256),)),
        "enc_bias": gaussian(key_list[3], (F,), 0.5, 3.0, ((0, 256),), jnp.float32),
        "dec_weight": gaussian(key_list[4], (F, TL * D), F ** -0.5, 0.03125, ((0, 4), (1, 64))),
        "dec_bias": gaussian(key_list[5], (TL * D,), 0.5, 3.0, ((0, 64),), jnp.float32),
    }


def column_blocks(left, right):
    width = right.shape[1]
    size = 1024 if width % 1024 == 0 else width
    count = width // size
    parts = right.reshape(right.shape[0], count, size).transpose(1, 0, 2)

    def one_block(part):
        return lax.dot_general(left, part, (((0,), (0,)), ((), ())), preferred_element_type=jnp.float32).astype(jnp.bfloat16)
    stacked = lax.map(one_block, parts)
    return stacked.transpose(1, 0, 2).reshape(left.shape[1], width)

def reference(sources, targets, enc_weight, enc_bias, dec_weight, dec_bias):
    preact = jnp.dot(sources, enc_weight, preferred_element_type=jnp.float32) + enc_bias
    feats = jax.nn.gelu(preact).astype(jnp.bfloat16)
    outputs = jnp.dot(feats, dec_weight, preferred_element_type=jnp.float32) + dec_bias
    misfit = outputs - targets.astype(jnp.float32)
    errors = (misfit * (1.0 / math.sqrt(TOKENS))).astype(jnp.bfloat16)
    mse = jnp.sum(misfit * misfit) / (TOKENS * TL * D)
    dec_grad = column_blocks(feats, errors)
    feat_grad = lax.dot_general(errors, dec_weight, (((1,), (1,)), ((), ())), preferred_element_type=jnp.float32)
    _, pullback = jax.vjp(jax.nn.gelu, preact)
    pre_grad = pullback(feat_grad)[0].astype(jnp.bfloat16)
    enc_grad = column_blocks(sources, pre_grad)
    return (enc_grad, dec_grad, mse)
```

```python
import math

import jax
import jax.numpy as jnp
from jax import lax
from jax.sharding import Mesh, PartitionSpec as P

LAYER = ("y", "x_lo", "z")
FEAT = ("x_hi", "core")


def spread_to(block, axes):
    n = lax.axis_size(axes)
    return lax.all_to_all(
        jnp.broadcast_to(block[None], (n, *block.shape)), axes, split_axis=0, concat_axis=0, tiled=True
    )


def per_device(sources, targets, enc_weight, enc_bias, dec_weight, dec_bias):
    n_y, n_xl, n_z = (lax.axis_size(a) for a in LAYER)
    n_xh, n_c = (lax.axis_size(a) for a in FEAT)
    n_layer = n_y * n_xl * n_z
    rows, width = dec_weight.shape
    feats_own = enc_weight.shape[1]
    depth = sources.shape[1]
    tokens = n_layer * n_xh * n_c
    factor = 1.0 / math.sqrt(tokens)

    owned = lax.all_to_all(targets.reshape(n_layer, 1, width), LAYER, split_axis=0, concat_axis=0, tiled=True)
    wanted = lax.all_gather(owned.reshape(n_layer, width), FEAT, axis=0, tiled=True)
    wanted = wanted.reshape(n_xh, n_c, n_y * n_xl, n_z, width).transpose(1, 2, 0, 3, 4).reshape(tokens, width)

    near = spread_to(sources, "z").reshape(n_z, depth)
    half = spread_to(near, ("y", "x_lo", "x_hi")).reshape(tokens // n_c, depth)
    inputs = spread_to(half, "core").reshape(tokens, depth)

    preact = jnp.dot(inputs, enc_weight, preferred_element_type=jnp.float32) + enc_bias
    preact = preact.T
    feats = jax.nn.gelu(preact).astype(jnp.bfloat16)

    near_feats = spread_to(feats, "z").reshape(n_z * feats_own, tokens)
    all_feats = spread_to(near_feats, ("y", "x_lo")).reshape(rows, tokens)
    partial_value = lax.dot_general(
        all_feats, dec_weight, (((0,), (0,)), ((), ())), preferred_element_type=jnp.float32
    ).astype(jnp.bfloat16)
    parts = lax.all_gather(partial_value, FEAT, axis=0)
    outputs = jnp.sum(parts.astype(jnp.float32), axis=0) + dec_bias
    misfit = outputs - wanted.astype(jnp.float32)
    errors = (misfit * factor).astype(jnp.bfloat16)

    own_sq = jnp.broadcast_to(jnp.sum(misfit * misfit), (n_layer, 1, 128))
    every_sq = lax.all_to_all(own_sq, LAYER, split_axis=0, concat_axis=0, tiled=True)
    mse = jnp.sum(every_sq[:, 0, 0]) / (tokens * n_layer * width)

    grads = lax.dot_general(
        dec_weight, errors, (((1,), (1,)), ((), ())), preferred_element_type=jnp.float32
    ).astype(jnp.bfloat16)
    far = lax.all_to_all(
        grads.reshape(n_y * n_xl, n_z * feats_own, tokens), ("y", "x_lo"), split_axis=0, concat_axis=0, tiled=True
    )
    far = jnp.sum(far.astype(jnp.float32), axis=0).astype(jnp.bfloat16)
    close = lax.all_to_all(
        far.reshape(n_z, feats_own, tokens), "z", split_axis=0, concat_axis=0, tiled=True
    )
    feat_grad = jnp.sum(close.astype(jnp.float32), axis=0)

    dec_grad = jnp.dot(all_feats, errors, preferred_element_type=jnp.float32).astype(jnp.bfloat16)
    _, pullback = jax.vjp(jax.nn.gelu, preact)
    pre_grad = pullback(feat_grad)[0].astype(jnp.bfloat16)
    enc_grad = lax.dot_general(
        inputs, pre_grad, (((0,), (1,)), ((), ())), preferred_element_type=jnp.float32
    ).astype(jnp.bfloat16)
    return (enc_grad, dec_grad, mse)


def solution(mesh):
    n_layer, n_feat = mesh.devices.shape
    n_x_lo, n_z = 2, 8
    torus = Mesh(
        mesh.devices.reshape(n_layer // (n_x_lo * n_z), n_x_lo, n_z, n_feat // 2, 2), (*LAYER, *FEAT)
    )
    return jax.shard_map(
        per_device,
        mesh=torus,
        in_specs=(
            P((*LAYER, *FEAT), None),
            P((*LAYER, *FEAT), None),
            P(None, (*FEAT, *LAYER)),
            P((*FEAT, *LAYER)),
            P(FEAT, LAYER),
            P(LAYER),
        ),
        out_specs=(P(None, (*FEAT, *LAYER)), P(FEAT, LAYER), P()),
        check_vma=False,
    )
```
